32 devices in a mesh: real: 2 (over y), comp: 4 (over z), space: 4 (over x, core).
Axes of the slice: x: 2, y: 2, z: 4, core: 2. Of those that a mesh axis runs over, the one named last changes fastest.
Arguments:
- concentration: float32 [256, 32, 2048], P(('real', 'comp'), None, 'space'), parts along dimension 0, may hold values from -12 to 12
- face_rate: float32 [2, 64, 2048], P(None, 'real', 'space'), parts along dimension 1, may hold values from 0.02 to 0.15
- face_flag: int32 [2, 64, 2048], P(None, 'real', 'space'), parts along dimension 1, may hold values from 0 to 1
- retardation: float32 [16], replicated, may hold values from 1 to 3
- dispersion: float32 [16], replicated, may hold values from 0.01 to 0.08
- mixing: float32 [16, 16], replicated, may hold values from -0.08 to 2.5
- mixing_inverse: float32 [16, 16], replicated, may hold values from -0.05 to 0.5
- affinity: float32 [16], replicated, may hold values from 0.5 to 3
- mineral: float32 [16], replicated, may hold values from 0.3 to 1.5
- stiff_mask: int32 [8, 64, 2048], P(None, ('real', 'comp'), 'space'), parts along dimension 1, may hold values from 0 to 1, as said below
Outputs:
- concentration_out: float32 [256, 32, 2048], P(('real', 'comp'), None, 'space'), parts along dimension 0
The draws below stay inside these ranges and needn't reach their ends.
There are 2 independent parts, one for each index of `real`. The reference program is written for one: setup_inputs(seed, part) draws one part's arguments, and reference() takes and returns one part's arrays. A program takes and returns all parts, laid end to end along the dimension named above; an argument that names none is the same for every part. Nothing has to cross between parts.
Inputs may be any that keep to these rules, and one draw needn't show every extreme that they name: `stiff_mask`: in every block of cells made of all 8 layers, x rows k * 8 to (k + 1) * 8 - 1 and y columns l * 512 to (l + 1) * 512 - 1, at most 8192 cells are stiff, and some block has exactly 8192.
All inputs are finite; a program needn't handle non-finite values.
Results may differ from the reference program's by a relative error of at most 0.00011.
Values sent between devices are 32-bit elements; how exact they have to be, the bound alone decides.
A program may use at most 64 MiB of HBM per device.

```python
import math
import jax
import jax.numpy as jnp
from jax import lax

NC = 16
NZ = 8
NY = 2048
XR = 8
STEPS = 2
NEWT = 4
STIFF = 4
NX = 32
NYD = 512
PLANES = 128
CELLS_DEV = 32768
CAP = 8192


def mixing_pair(key):
    folded = jax.random.fold_in(key, 17)
    key_off, key_diag = jax.random.split(folded)
    off_diagonal = jax.random.uniform(key_off, (NC, NC), jnp.float32, -0.08, 0.08) * (1.0 - jnp.eye(NC, dtype=jnp.float32))
    diagonal = jax.random.uniform(key_diag, (NC,), jnp.float32, 1.5, 2.5)
    return off_diagonal + jnp.diag(diagonal)


def draw_mixing(key, part):
    return mixing_pair(key)


def draw_mixing_inverse(key, part):
    return jnp.linalg.inv(mixing_pair(key) + 3.0 * jnp.eye(NC, dtype=jnp.float32))


def draw_stiff_mask(key, part):
    row_blocks = NX // XR
    column_blocks = NY // NYD
    block_count = row_blocks * column_blocks
    key_heavy, key_light, key_chosen, key_ranks = jax.random.split(key, 4)
    heavy_flag = jax.random.randint(key_heavy, (block_count,), 0, 4) == 0
    light_counts = jax.random.randint(key_light, (block_count,), CAP // 8, CAP // 3 + 1)
    counts = jnp.where(heavy_flag, CAP, light_counts)
    chosen = jax.random.randint(key_chosen, (), 0, block_count)
    counts = jnp.where(jnp.arange(block_count) == chosen, CAP, counts)
    block_keys = jax.random.split(key_ranks, block_count)
    ranking = jax.vmap(lambda subkey: jax.random.permutation(subkey, CELLS_DEV))(block_keys)
    marked = (ranking < counts[:, None]).astype(jnp.int32)
    marked = marked.reshape(row_blocks, column_blocks, NZ, XR, NYD).transpose(2, 0, 3, 1, 4)
    return marked.reshape(NZ, NX, NY)


def touch_ends(drawn, key, least, high):
    shape = drawn.shape
    index_at = [jax.random.randint(jax.random.fold_in(key, axis), (), 0, shape[axis]) for axis in range(len(shape))]
    drawn = drawn.at[tuple(index_at)].set(least)
    longest = shape.index(max(shape))
    index_at[longest] = (index_at[longest] + 1) % shape[longest]
    return drawn.at[tuple(index_at)].set(high)


def shard_levels(own_key, shape, shards, least, high):
    factor_of, own = 1.0, jax.random.fold_in(own_key, 6)
    for position, parts in shards:
        steps = jnp.exp(jax.random.uniform(jax.random.fold_in(own, position), (parts,), jnp.float32, least / len(shards), high / len(shards)))
        factor_of = factor_of * jnp.repeat(steps, shape[position] // parts).reshape([-1 if axis == position else 1 for axis in range(len(shape))])
    return factor_of


def noise(key, extent, deviation, reach, cuts=(), kind=jnp.bfloat16):
    drawn = deviation * jax.random.normal(key, extent, jnp.float32)
    if cuts:
        drawn = drawn * shard_levels(key, extent, cuts, -0.22, 0.18)
    return jnp.clip(drawn, -reach, reach).astype(kind)


def setup_inputs(seed: int = 0, part: int = 0) -> dict:
    seeds = jax.random.split(jax.random.key(seed), 11)
    part_keys = jax.random.split(jax.random.fold_in(seeds[10], part), 11)
    return {
        "concentration": noise(part_keys[0], (PLANES, NX, NY), 2.0, 12.0, ((0, 4), (2, 4)), jnp.float32),
        "face_rate": jnp.clip(jnp.exp(math.log(0.15) - 2.014903 * jax.random.uniform(part_keys[1], (2, NX, NY), jnp.float32) ** shard_levels(part_keys[1], (2, NX, NY), ((2, 4),), -0.2, 0.2)), 0.02, 0.15),
        "face_flag": touch_ends(jax.random.randint(part_keys[2], (2, NX, NY), 0, 2), jax.random.fold_in(part_keys[2], 1), 0, 1).astype(jnp.int32),
        "retardation": jnp.clip(jnp.exp(jax.random.uniform(seeds[3], (NC,), jnp.float32, math.log(1.0), math.log(3.0))), 1.0, 3.0),
        "dispersion": jnp.clip(jnp.exp(jax.random.uniform(seeds[4], (NC,), jnp.float32, math.log(0.01), math.log(0.08))), 0.01, 0.08),
        "mixing": draw_mixing(jax.random.fold_in(seeds[10], 71), part),
        "mixing_inverse": draw_mixing_inverse(jax.random.fold_in(seeds[10], 71), part),
        "affinity": jnp.clip(jnp.exp(jax.random.uniform(seeds[7], (NC,), jnp.float32, math.log(0.5), math.log(3.0))), 0.5, 3.0),
        "mineral": jnp.clip(jnp.exp(jax.random.uniform(seeds[8], (NC,), jnp.float32, math.log(0.3), math.log(1.5))), 0.3, 1.5),
        "stiff_mask": draw_stiff_mask(jax.random.fold_in(jax.random.fold_in(seeds[10], part), 71), part),
    }


highest = lax.Precision.HIGHEST

def shift_down(values, axis_index):
    size_along = values.shape[axis_index]
    zero_row = jnp.zeros_like(lax.slice_in_dim(values, 0, 1, axis=axis_index))
    kept = lax.slice_in_dim(values, 0, size_along - 1, axis=axis_index)
    return jnp.concatenate([zero_row, kept], axis=axis_index)

def shift_up(values, axis_index):
    size_along = values.shape[axis_index]
    zero_row = jnp.zeros_like(lax.slice_in_dim(values, 0, 1, axis=axis_index))
    kept = lax.slice_in_dim(values, 1, size_along, axis=axis_index)
    return jnp.concatenate([kept, zero_row], axis=axis_index)

def face_weights(face_rate, face_flag):
    flag_values = face_flag.astype(jnp.float32)
    weight_plus = face_rate * flag_values
    weight_minus = face_rate * (1.0 - flag_values)
    return (weight_plus, weight_minus)

def advance(values, lower_row, upper_row, lower_col, upper_col, coefficients, retard_planes, spread_planes):
    divergence = coefficients[0] * lower_row + coefficients[1] * upper_row + coefficients[2] * lower_col + coefficients[3] * upper_col - coefficients[4] * values
    laplace = lower_row + upper_row + lower_col + upper_col - 4.0 * values
    return values + (divergence + spread_planes * laplace) / retard_planes

def residual_of(species, target, mixing, affinity, mineral, stiff):
    total = jnp.dot(mixing.astype(jnp.float32), species.astype(jnp.float32), precision=highest, preferred_element_type=jnp.float32) + affinity[:, None] * jnp.tanh(species)
    if stiff:
        total = total + mineral[:, None] * jnp.tanh(2.0 * species)
    return total - target

def newton_steps(species, target, repeats, stiff, mixing, mixing_inverse, affinity, mineral):
    for iteration in range(repeats):
        update = residual_of(species, target, mixing, affinity, mineral, stiff)
        species = species - jnp.dot(mixing_inverse.astype(jnp.float32), update.astype(jnp.float32), precision=highest, preferred_element_type=jnp.float32)
    return species

def reference(concentration, face_rate, face_flag, retardation, dispersion, mixing, mixing_inverse, affinity, mineral, stiff_mask):
    weight_plus, weight_minus = face_weights(face_rate, face_flag)
    down_plus = shift_down(weight_plus[0], 0)
    down_minus = shift_down(weight_minus[0], 0)
    side_plus = shift_down(weight_plus[1], 1)
    side_minus = shift_down(weight_minus[1], 1)
    centre = down_minus + weight_plus[0] + side_minus + weight_plus[1]
    coefficients = jnp.stack([down_plus, weight_minus[0], side_plus, weight_minus[1], centre])
    flat_mask = stiff_mask.reshape(-1) > 0

    def one_component(packed):
        component_planes, retard_value, spread_value = packed
        return advance(component_planes, shift_down(component_planes, 1), shift_up(component_planes, 1), shift_down(component_planes, 2), shift_up(component_planes, 2), coefficients, retard_value, spread_value)
    values = concentration
    for step_index in range(STEPS):
        layered = values.reshape(NC, NZ, NX, NY)
        layered = lax.map(one_component, (layered, retardation, dispersion))
        target = layered.reshape(NC, NZ * NX * NY)
        species = jnp.zeros_like(target)
        species = newton_steps(species, target, NEWT, False, mixing, mixing_inverse, affinity, mineral)
        stiffer = newton_steps(species, target, STIFF, True, mixing, mixing_inverse, affinity, mineral)
        species = jnp.where(flat_mask[None, :], stiffer, species)
        values = species.reshape(PLANES, NX, NY)
    return values
```

```python
import functools

import jax
import jax.numpy as jnp
from jax import lax
from jax.experimental import pallas as pl
from jax.experimental.pallas import tpu as pltpu
from jax.sharding import PartitionSpec as P

NC = 16
NZ = 8
STEPS = 2
NEWT = 4
STIFF = 4
LANES = 128
AHEAD = 3
BEHIND = 2
MESH = pl.DeviceIdType.MESH

highest = lax.Precision.HIGHEST


def split(value):
    high = value.astype(jnp.bfloat16)
    low = (value - high.astype(jnp.float32)).astype(jnp.bfloat16)
    return high, low


def expand(small, rows):
    count = small.shape[0]
    size = count * rows
    tall = (
        lax.broadcasted_iota(jnp.int32, (size, count), 0) // rows
        == lax.broadcasted_iota(jnp.int32, (size, count), 1)
    ).astype(jnp.float32)
    wide = (
        lax.broadcasted_iota(jnp.int32, (count, size), 1) // rows
        == lax.broadcasted_iota(jnp.int32, (count, size), 0)
    ).astype(jnp.float32)
    dot = functools.partial(jnp.dot, precision=highest, preferred_element_type=jnp.float32)
    full = dot(dot(tall, small), wide)
    same = (
        lax.broadcasted_iota(jnp.int32, (size, size), 0) % rows
        == lax.broadcasted_iota(jnp.int32, (size, size), 1) % rows
    )
    return jnp.where(same, full, 0.0)


def shift_cols(values, left, right):
    columns = values.shape[1]
    lower = pltpu.roll(jnp.concatenate([left, values], axis=1), 1, 1)[:, LANES:]
    upper = pltpu.roll(
        jnp.concatenate([values, right], axis=1), columns + LANES - 1, 1
    )[:, :columns]
    return lower, upper


def stencil(values, lower_row, upper_row, lower_col, upper_col, coefs, spread, retard):
    inverse = 1.0 / jnp.full((1, values.shape[1]), retard, jnp.float32)
    moved = (
        (coefs[0] + spread) * lower_row
        + (coefs[1] + spread) * upper_row
        + (coefs[2] + spread) * lower_col
        + (coefs[3] + spread) * upper_col
        - (coefs[4] + 4.0 * spread) * values
    )
    return values + moved * inverse


def fused_kernel(
    n,
    wide,
    conc,
    rate,
    flag,
    retard,
    spread,
    mixing,
    inverse,
    affinity,
    mineral,
    mask,
    out,
    moved,
    cell,
    first,
    second,
    xsend,
    xrecv,
    yone,
    ytwo,
    rim_rate,
    rim_flag,
    coefs,
    weights_in,
    weights_one,
    weights_two,
    target,
    state,
    base,
    kept,
    in_send,
    in_recv,
    out_send,
    out_recv,
    x_send,
    x_recv,
    y1_send,
    y1_recv,
    y2_send,
    y2_recv,
    r_send,
    r_recv,
):
    own, layers, nx, ny = conc.shape
    rows = mask.shape[1]
    me = lax.axis_index("comp")
    side = lax.axis_index("space")
    has_left, has_right = side > 0, side < wide - 1
    has_low, has_up = me > 0, me < n - 1
    my_rows = pl.ds(pl.multiple_of(me * rows, rows), rows)

    def peer(d):
        return lax.rem(me + d, n)

    def remote(src, dst, send, recv, **where):
        return pltpu.make_async_remote_copy(
            src_ref=src, dst_ref=dst, send_sem=send, recv_sem=recv,
            device_id=where, device_id_type=MESH,
        )

    def y1_copy(z, way):
        source = conc.at[:, z, :, pl.ds(ny - LANES if way == 0 else 0, LANES)]
        return remote(source, yone.at[way, :, z], y1_send.at[way, z], y1_recv.at[way, z],
                      space=side + (1 if way == 0 else -1))

    def y2_copy(z, way):
        source = first.at[:, z, :, pl.ds(ny - LANES if way == 0 else 0, LANES)]
        return remote(source, ytwo.at[way, :, z], y2_send.at[way, z], y2_recv.at[way, z],
                      space=side + (1 if way == 0 else -1))

    def x_copy(z, way):
        return remote(xsend.at[way, z], xrecv.at[way, z], x_send.at[way, z], x_recv.at[way, z],
                      comp=me + (1 if way == 0 else -1))

    def rim_copies():
        last = pl.ds(ny - LANES, LANES)
        return (
            remote(rate.at[1, :, last], rim_rate, r_send.at[0], r_recv.at[0], space=side + 1),
            remote(flag.at[1, :, last], rim_flag, r_send.at[1], r_recv.at[1], space=side + 1),
        )

    def in_copy(z, d):
        to = peer(d)
        source = moved.at[:, z, pl.ds(pl.multiple_of(to * rows, rows), rows), :]
        return remote(source, cell.at[pl.ds(me * own, own), z],
                      in_send.at[z, d - 1], in_recv.at[z, d - 1], comp=to)

    def in_arrival(z, d):
        source = moved.at[:, z, my_rows, :]
        return remote(source, cell.at[pl.ds(peer(n - d) * own, own), z],
                      in_send.at[z, d - 1], in_recv.at[z, d - 1], comp=peer(d))

    def out_copy(z, d):
        to = peer(d)
        return remote(second.at[pl.ds(to * own, own), z], out.at[:, z, my_rows, :],
                      out_send.at[z, d - 1], out_recv.at[z, d - 1], comp=to)

    def out_arrival(z, d):
        rows_from = pl.ds(pl.multiple_of(peer(n - d) * rows, rows), rows)
        return remote(second.at[pl.ds(me * own, own), z], out.at[:, z, rows_from, :],
                      out_send.at[z, d - 1], out_recv.at[z, d - 1], comp=peer(d))

    barrier = pltpu.get_barrier_semaphore()
    for d in range(1, n):
        pl.semaphore_signal(barrier, inc=1, device_id={"comp": peer(d)}, device_id_type=MESH)

    @pl.when(has_left)
    def _():
        pl.semaphore_signal(barrier, inc=1, device_id={"space": side - 1}, device_id_type=MESH)

    @pl.when(has_right)
    def _():
        pl.semaphore_signal(barrier, inc=1, device_id={"space": side + 1}, device_id_type=MESH)

    pl.semaphore_wait(barrier, n - 1 + has_left.astype(jnp.int32) + has_right.astype(jnp.int32))

    @pl.when(has_right)
    def _():
        for copy in rim_copies():
            copy.start()

        @pl.loop(0, layers)
        def _(z):
            y1_copy(z, 0).start()

    @pl.when(has_left)
    def _():
        @pl.loop(0, layers)
        def _(z):
            y1_copy(z, 1).start()

    @pl.when(jnp.logical_not(has_left))
    def _():
        yone[0] = jnp.zeros_like(yone[0])
        ytwo[0] = jnp.zeros_like(ytwo[0])
        rim_rate[...] = jnp.zeros_like(rim_rate)
        rim_flag[...] = jnp.zeros_like(rim_flag)

    @pl.when(jnp.logical_not(has_right))
    def _():
        yone[1] = jnp.zeros_like(yone[1])
        ytwo[1] = jnp.zeros_like(ytwo[1])

    @pl.when(jnp.logical_not(has_low))
    def _():
        xrecv[0] = jnp.zeros_like(xrecv[0])

    @pl.when(jnp.logical_not(has_up))
    def _():
        xrecv[1] = jnp.zeros_like(xrecv[1])

    @pl.when(has_left)
    def _():
        for copy in rim_copies():
            copy.wait_recv()

    flags = flag[...].astype(jnp.float32)
    plus = rate[...] * flags
    minus = rate[...] * (1.0 - flags)
    rim = rim_flag[...].astype(jnp.float32)
    rim_plus = rim_rate[...] * rim
    rim_minus = rim_rate[...] * (1.0 - rim)
    row_index = lax.broadcasted_iota(jnp.int32, (nx, ny), 0)
    down_plus = jnp.where(row_index == 0, 0.0, pltpu.roll(plus[0], 1, 0))
    down_minus = jnp.where(row_index == 0, 0.0, pltpu.roll(minus[0], 1, 0))
    side_plus = pltpu.roll(jnp.concatenate([rim_plus, plus[1]], axis=1), 1, 1)[:, LANES:]
    side_minus = pltpu.roll(jnp.concatenate([rim_minus, minus[1]], axis=1), 1, 1)[:, LANES:]
    coefs[0] = down_plus
    coefs[1] = minus[0]
    coefs[2] = side_plus
    coefs[3] = minus[1]
    coefs[4] = down_minus + plus[0] + side_minus + plus[1]

    def build_weights():
        matrix = inverse[...]
        eye = (
            lax.broadcasted_iota(jnp.int32, matrix.shape, 0)
            == lax.broadcasted_iota(jnp.int32, matrix.shape, 1)
        ).astype(jnp.float32)
        carry = eye - jnp.dot(
            matrix, mixing[...], precision=highest, preferred_element_type=jnp.float32
        )
        parts = [carry, -matrix * affinity[...], -matrix * mineral[...], matrix]
        parts = [split(expand(part, rows)) for part in parts]
        for ref, chosen in (
            (weights_one, parts[:2]),
            (weights_two, parts[:3]),
            (weights_in, parts[3:]),
        ):
            high = [part[0] for part in chosen]
            low = [part[1] for part in chosen]
            ref[...] = jnp.concatenate(high + high + low, axis=1)

    def product(ref, values):
        pairs = [split(value) for value in values]
        high = [pair[0] for pair in pairs]
        low = [pair[1] for pair in pairs]
        data = jnp.concatenate(high + low + high, axis=0)
        return jnp.dot(ref[...], data, preferred_element_type=jnp.float32)

    width = min(256, ny)
    pieces = [pl.ds(start, width) for start in range(0, ny, width)]

    def speciate(z):
        for piece in pieces:
            begun = product(weights_in, [target[:, piece]])
            base[:, piece] = begun
            state[:, piece] = begun

        @pl.loop(0, NEWT - 1)
        def _(_step):
            for piece in pieces:
                s = state[:, piece]
                state[:, piece] = base[:, piece] + product(weights_one, [s, jnp.tanh(s)])

        kept[...] = state[...]

        @pl.loop(0, STIFF)
        def _(_step):
            for piece in pieces:
                s = state[:, piece]
                state[:, piece] = base[:, piece] + product(
                    weights_two, [s, jnp.tanh(s), jnp.tanh(2.0 * s)]
                )

        stiff = mask[z] > 0
        return [
            jnp.where(stiff, state[pl.ds(c * rows, rows), :], kept[pl.ds(c * rows, rows), :])
            for c in range(NC)
        ]

    def stage_a(z):
        @pl.when(has_left)
        def _():
            y1_copy(z, 0).wait_recv()

        @pl.when(has_right)
        def _():
            y1_copy(z, 1).wait_recv()

        for c in range(own):
            u = conc[c, z]
            lower_row = jnp.where(row_index == 0, 0.0, pltpu.roll(u, 1, 0))
            upper_row = jnp.where(row_index == nx - 1, 0.0, pltpu.roll(u, nx - 1, 0))
            lower_col, upper_col = shift_cols(u, yone[0, c, z], yone[1, c, z])
            component = me * own + c
            moved[c, z] = stencil(
                u, lower_row, upper_row, lower_col, upper_col,
                [coefs[k] for k in range(5)], spread[component], retard[component],
            )
        for d in range(1, n):
            in_copy(z, d).start()

    def stage_b(z):
        for d in range(1, n):
            in_arrival(z, d).wait_recv()
        for c in range(NC):
            target[pl.ds(c * rows, rows), :] = cell[c, z]
        for c in range(own):
            spot = pl.multiple_of((me * own + c) * rows, rows)
            target[pl.ds(spot, rows), :] = moved[c, z, my_rows, :]
        done = speciate(z)
        for c in range(NC):
            first[c, z] = done[c]
            xsend[0, z, pl.ds(c, 1), :] = done[c][rows - 1 : rows]
            xsend[1, z, pl.ds(c, 1), :] = done[c][:1]

        @pl.when(has_up)
        def _():
            x_copy(z, 0).start()

        @pl.when(has_low)
        def _():
            x_copy(z, 1).start()

        @pl.when(has_right)
        def _():
            y2_copy(z, 0).start()

        @pl.when(has_left)
        def _():
            y2_copy(z, 1).start()

    def stage_c(z):
        @pl.when(has_low)
        def _():
            x_copy(z, 0).wait_recv()

        @pl.when(has_up)
        def _():
            x_copy(z, 1).wait_recv()

        @pl.when(has_left)
        def _():
            y2_copy(z, 0).wait_recv()

        @pl.when(has_right)
        def _():
            y2_copy(z, 1).wait_recv()

        local = lax.broadcasted_iota(jnp.int32, (rows, ny), 0)
        for c in range(NC):
            u = first[c, z]
            below = jnp.broadcast_to(xrecv[0, z, pl.ds(c, 1), :], u.shape)
            above = jnp.broadcast_to(xrecv[1, z, pl.ds(c, 1), :], u.shape)
            lower_row = jnp.where(local == 0, below, pltpu.roll(u, 1, 0))
            upper_row = jnp.where(local == rows - 1, above, pltpu.roll(u, rows - 1, 0))
            lower_col, upper_col = shift_cols(u, ytwo[0, c, z], ytwo[1, c, z])
            target[pl.ds(c * rows, rows), :] = stencil(
                u, lower_row, upper_row, lower_col, upper_col,
                [coefs[k, my_rows, :] for k in range(5)], spread[c], retard[c],
            )
        done = speciate(z)
        for c in range(NC):
            second[c, z] = done[c]
        for d in range(1, n):
            out_copy(z, d).start()
        for c in range(own):
            out[c, z, my_rows, :] = second[me * own + c, z]

    @pl.loop(0, layers + AHEAD + BEHIND)
    def _(i):
        @pl.when(i < layers)
        def _():
            stage_a(i)

        @pl.when(i == AHEAD - 1)
        def _():
            build_weights()

        @pl.when((i >= AHEAD) & (i < layers + AHEAD))
        def _():
            stage_b(i - AHEAD)

        @pl.when(i >= AHEAD + BEHIND)
        def _():
            stage_c(i - AHEAD - BEHIND)

    @pl.loop(0, layers)
    def _(z):
        for d in range(1, n):
            out_arrival(z, d).wait_recv()
            in_copy(z, d).wait_send()
            out_copy(z, d).wait_send()

    @pl.when(has_right)
    def _():
        for copy in rim_copies():
            copy.wait_send()

        @pl.loop(0, layers)
        def _(z):
            y1_copy(z, 0).wait_send()
            y2_copy(z, 0).wait_send()

    @pl.when(has_left)
    def _():
        @pl.loop(0, layers)
        def _(z):
            y1_copy(z, 1).wait_send()
            y2_copy(z, 1).wait_send()

    @pl.when(has_up)
    def _():
        @pl.loop(0, layers)
        def _(z):
            x_copy(z, 0).wait_send()

    @pl.when(has_low)
    def _():
        @pl.loop(0, layers)
        def _(z):
            x_copy(z, 1).wait_send()


def fused_shards(
    n, wide, concentration, face_rate, face_flag, retardation, dispersion,
    mixing, mixing_inverse, affinity, mineral, stiff_mask,
):
    planes, nx, ny = concentration.shape
    own = planes // NZ
    rows = stiff_mask.shape[1]
    size = NC * rows
    f32, bf16 = jnp.float32, jnp.bfloat16
    vmem = pl.BlockSpec(memory_space=pltpu.VMEM)
    smem = pl.BlockSpec(memory_space=pltpu.SMEM)
    dma = pltpu.SemaphoreType.DMA
    result = pl.pallas_call(
        functools.partial(fused_kernel, n, wide),
        out_shape=jax.ShapeDtypeStruct((own, NZ, nx, ny), f32),
        in_specs=[vmem, vmem, vmem, smem, smem, vmem, vmem, vmem, vmem, vmem],
        out_specs=vmem,
        scratch_shapes=[
            pltpu.VMEM((own, NZ, nx, ny), f32),
            pltpu.VMEM((NC, NZ, rows, ny), f32),
            pltpu.VMEM((NC, NZ, rows, ny), f32),
            pltpu.VMEM((NC, NZ, rows, ny), f32),
            pltpu.VMEM((2, NZ, NC, ny), f32),
            pltpu.VMEM((2, NZ, NC, ny), f32),
            pltpu.VMEM((2, own, NZ, nx, LANES), f32),
            pltpu.VMEM((2, NC, NZ, rows, LANES), f32),
            pltpu.VMEM((nx, LANES), f32),
            pltpu.VMEM((nx, LANES), jnp.int32),
            pltpu.VMEM((5, nx, ny), f32),
            pltpu.VMEM((size, 3 * size), bf16),
            pltpu.VMEM((size, 6 * size), bf16),
            pltpu.VMEM((size, 9 * size), bf16),
            pltpu.VMEM((size, ny), f32),
            pltpu.VMEM((size, ny), f32),
            pltpu.VMEM((size, ny), f32),
            pltpu.VMEM((size, ny), f32),
            dma((NZ, n - 1)), dma((NZ, n - 1)),
            dma((NZ, n - 1)), dma((NZ, n - 1)),
            dma((2, NZ)), dma((2, NZ)),
            dma((2, NZ)), dma((2, NZ)),
            dma((2, NZ)), dma((2, NZ)),
            dma((2,)), dma((2,)),
        ],
        compiler_params=pltpu.CompilerParams(collective_id=0, has_side_effects=True),
    )(
        concentration.reshape(own, NZ, nx, ny), face_rate, face_flag, retardation, dispersion,
        mixing, mixing_inverse, affinity.reshape(1, NC), mineral.reshape(1, NC), stiff_mask,
    )
    return result.reshape(planes, nx, ny)


def shifted(shard, axis, by):
    devices = lax.axis_size(axis)
    pairs = [(i, i + by) for i in range(devices) if 0 <= i + by < devices]
    return lax.ppermute(shard, axis, pairs)


def extended(block, sides, width):
    for axis, dim in sides:
        count = lax.axis_size(axis)
        forward = [(i, i + 1) for i in range(count - 1)]
        backward = [(target, source) for source, target in forward]
        low = lax.ppermute(
            lax.slice_in_dim(block, block.shape[dim] - width, None, axis=dim), axis, forward
        )
        high = lax.ppermute(lax.slice_in_dim(block, 0, width, axis=dim), axis, backward)
        block = jnp.concatenate([low, block, high], axis=dim)
    return block


def shift_down(values, axis_index):
    size_along = values.shape[axis_index]
    zero_row = jnp.zeros_like(lax.slice_in_dim(values, 0, 1, axis=axis_index))
    kept = lax.slice_in_dim(values, 0, size_along - 1, axis=axis_index)
    return jnp.concatenate([zero_row, kept], axis=axis_index)


def face_weights(face_rate, face_flag):
    flag_values = face_flag.astype(jnp.float32)
    weight_plus = face_rate * flag_values
    weight_minus = face_rate * (1.0 - flag_values)
    return (weight_plus, weight_minus)


def advance(
    values, lower_row, upper_row, lower_col, upper_col, coefficients, retard_planes, spread_planes
):
    divergence = (
        coefficients[0] * lower_row
        + coefficients[1] * upper_row
        + coefficients[2] * lower_col
        + coefficients[3] * upper_col
        - coefficients[4] * values
    )
    laplace = lower_row + upper_row + lower_col + upper_col - 4.0 * values
    return values + (divergence + spread_planes * laplace) / retard_planes


def residual_of(species, target, mixing, affinity, mineral, stiff):
    total = jnp.dot(
        mixing, species, precision=highest, preferred_element_type=jnp.float32
    ) + affinity[:, None] * jnp.tanh(species)
    if stiff:
        total = total + mineral[:, None] * jnp.tanh(2.0 * species)
    return total - target


def newton_steps(species, target, repeats, stiff, mixing, mixing_inverse, affinity, mineral):
    for iteration in range(repeats):
        update = residual_of(species, target, mixing, affinity, mineral, stiff)
        species = species - jnp.dot(
            mixing_inverse, update, precision=highest, preferred_element_type=jnp.float32
        )
    return species


def speciate(cell_block, stiff_mask, mixing, mixing_inverse, affinity, mineral):
    target = cell_block.reshape(NC, -1)
    flat_mask = stiff_mask.reshape(-1) > 0
    species = jnp.zeros_like(target)
    species = newton_steps(species, target, NEWT, False, mixing, mixing_inverse, affinity, mineral)
    stiffer = newton_steps(species, target, STIFF, True, mixing, mixing_inverse, affinity, mineral)
    species = jnp.where(flat_mask[None, :], stiffer, species)
    return species.reshape(cell_block.shape)


def shards(
    concentration,
    face_rate,
    face_flag,
    retardation,
    dispersion,
    mixing,
    mixing_inverse,
    affinity,
    mineral,
    stiff_mask,
):
    weight_plus, weight_minus = face_weights(face_rate, face_flag)
    rim_weights = jnp.stack([weight_plus[1, :, -1], weight_minus[1, :, -1]])
    left_rims = shifted(rim_weights, "space", 1)
    side_plus = jnp.concatenate([left_rims[0][:, None], weight_plus[1, :, :-1]], axis=1)
    side_minus = jnp.concatenate([left_rims[1][:, None], weight_minus[1, :, :-1]], axis=1)
    down_plus = shift_down(weight_plus[0], 0)
    down_minus = shift_down(weight_minus[0], 0)
    centre = down_minus + weight_plus[0] + side_minus + weight_plus[1]
    coefficients = jnp.stack([down_plus, weight_minus[0], side_plus, weight_minus[1], centre])
    retard_all = jnp.repeat(retardation, NZ)
    spread_all = jnp.repeat(dispersion, NZ)
    rows_held = stiff_mask.shape[1]
    row_start = lax.axis_index("comp") * rows_held
    cell_coefficients = lax.dynamic_slice_in_dim(coefficients, row_start, rows_held, 1)
    retard_planes = retard_all[:, None, None]
    spread_planes = spread_all[:, None, None]
    cell_block = lax.all_to_all(concentration, "comp", split_axis=1, concat_axis=0, tiled=True)
    for step_index in range(STEPS):
        padded = extended(cell_block, (("comp", 1), ("space", 2)), 1)
        cell_block = advance(
            cell_block,
            padded[:, :-2, 1:-1],
            padded[:, 2:, 1:-1],
            padded[:, 1:-1, :-2],
            padded[:, 1:-1, 2:],
            cell_coefficients,
            retard_planes,
            spread_planes,
        )
        cell_block = speciate(cell_block, stiff_mask, mixing, mixing_inverse, affinity, mineral)
    return lax.all_to_all(cell_block, "comp", split_axis=0, concat_axis=1, tiled=True)


def solution(mesh):
    in_specs = (
        P(("real", "comp"), None, "space"),
        P(None, "real", "space"),
        P(None, "real", "space"),
        P(),
        P(),
        P(),
        P(),
        P(),
        P(),
        P(None, ("real", "comp"), "space"),
    )
    out_specs = P(("real", "comp"), None, "space")
    n, wide = mesh.shape["comp"], mesh.shape["space"]
    body = functools.partial(fused_shards, n, wide) if NC % n == 0 else shards
    return jax.shard_map(body, mesh=mesh, in_specs=in_specs, out_specs=out_specs, check_vma=False)
```

```python
import functools

import jax
import jax.numpy as jnp
from jax import lax
from jax.experimental import pallas as pl
from jax.experimental.pallas import tpu as pltpu
from jax.sharding import PartitionSpec as P

NC = 16
NZ = 8
STEPS = 2
NEWT = 4
STIFF = 4
LANES = 128
AHEAD = 3
BEHIND = 2
MESH = pl.DeviceIdType.MESH

highest = lax.Precision.HIGHEST


def split(value):
    high = value.astype(jnp.bfloat16)
    low = (value - high.astype(jnp.float32)).astype(jnp.bfloat16)
    return high, low


def expand(small, rows):
    count = small.shape[0]
    size = count * rows
    tall = (
        lax.broadcasted_iota(jnp.int32, (size, count), 0) // rows
        == lax.broadcasted_iota(jnp.int32, (size, count), 1)
    ).astype(jnp.float32)
    wide = (
        lax.broadcasted_iota(jnp.int32, (count, size), 1) // rows
        == lax.broadcasted_iota(jnp.int32, (count, size), 0)
    ).astype(jnp.float32)
    dot = functools.partial(jnp.dot, precision=highest, preferred_element_type=jnp.float32)
    full = dot(dot(tall, small), wide)
    same = (
        lax.broadcasted_iota(jnp.int32, (size, size), 0) % rows
        == lax.broadcasted_iota(jnp.int32, (size, size), 1) % rows
    )
    return jnp.where(same, full, 0.0)


def shift_cols(values, left, right):
    columns = values.shape[1]
    lower = pltpu.roll(jnp.concatenate([left, values], axis=1), 1, 1)[:, LANES:]
    upper = pltpu.roll(
        jnp.concatenate([values, right], axis=1), columns + LANES - 1, 1
    )[:, :columns]
    return lower, upper


def stencil(values, lower_row, upper_row, lower_col, upper_col, coefs, spread, retard):
    inverse = 1.0 / jnp.full((1, values.shape[1]), retard, jnp.float32)
    moved = (
        (coefs[0] + spread) * lower_row
        + (coefs[1] + spread) * upper_row
        + (coefs[2] + spread) * lower_col
        + (coefs[3] + spread) * upper_col
        - (coefs[4] + 4.0 * spread) * values
    )
    return values + moved * inverse


def fused_kernel(
    n,
    wide,
    conc_hbm,
    rate_hbm,
    flag_hbm,
    retard,
    spread,
    mixing,
    inverse,
    affinity,
    mineral,
    mask_hbm,
    out,
    conc,
    rate,
    flag,
    mask,
    moved,
    cell,
    first,
    second,
    xsend,
    xrecv,
    yone,
    ytwo,
    rim_rate,
    rim_flag,
    coefs,
    weights_in,
    weights_one,
    weights_two,
    target,
    state,
    base,
    kept,
    in_send,
    in_recv,
    out_send,
    out_recv,
    x_send,
    x_recv,
    y1_send,
    y1_recv,
    y2_send,
    y2_recv,
    r_send,
    r_recv,
    load_sem,
    small_sem,
):
    own, layers, nx, ny = conc.shape
    rows = mask.shape[1]
    me = lax.axis_index("comp")
    side = lax.axis_index("space")
    has_left, has_right = side > 0, side < wide - 1
    has_low, has_up = me > 0, me < n - 1
    my_rows = pl.ds(pl.multiple_of(me * rows, rows), rows)

    def peer(d):
        if n == 4:
            return (lax.rem(me + 2, 4), 3 - me, me + 1 - 2 * lax.rem(me, 2))[d - 1]
        return lax.rem(me + d, n)

    def source_of(d):
        return peer(d) if n == 4 else lax.rem(me + n - d, n)

    def load(z):
        return pltpu.make_async_copy(conc_hbm.at[:, z], conc.at[:, z], load_sem.at[z])

    smalls = [
        pltpu.make_async_copy(rate_hbm, rate, small_sem.at[0]),
        pltpu.make_async_copy(flag_hbm, flag, small_sem.at[1]),
        pltpu.make_async_copy(mask_hbm, mask, small_sem.at[2]),
    ]

    def remote(src, dst, send, recv, **where):
        return pltpu.make_async_remote_copy(
            src_ref=src, dst_ref=dst, send_sem=send, recv_sem=recv,
            device_id=where, device_id_type=MESH,
        )

    def y1_copy(z, way):
        source = conc_hbm.at[:, z, :, pl.ds(ny - LANES if way == 0 else 0, LANES)]
        return remote(source, yone.at[way, :, z], y1_send.at[way, z], y1_recv.at[way, z],
                      space=side + (1 if way == 0 else -1))

    def y2_copy(z, way):
        source = first.at[:, z, :, pl.ds(ny - LANES if way == 0 else 0, LANES)]
        return remote(source, ytwo.at[way, :, z], y2_send.at[way, z], y2_recv.at[way, z],
                      space=side + (1 if way == 0 else -1))

    def x_copy(z, way):
        return remote(xsend.at[way, z], xrecv.at[way, z], x_send.at[way, z], x_recv.at[way, z],
                      comp=me + (1 if way == 0 else -1))

    def rim_copies():
        last = pl.ds(ny - LANES, LANES)
        return (
            remote(rate_hbm.at[1, :, last], rim_rate, r_send.at[0], r_recv.at[0], space=side + 1),
            remote(flag_hbm.at[1, :, last], rim_flag, r_send.at[1], r_recv.at[1], space=side + 1),
        )

    def in_copy(z, d):
        to = peer(d)
        source = moved.at[:, z, pl.ds(pl.multiple_of(to * rows, rows), rows), :]
        return remote(source, cell.at[pl.ds(me * own, own), z],
                      in_send.at[z, d - 1], in_recv.at[z, d - 1], comp=to)

    def in_arrival(z, d):
        source = moved.at[:, z, my_rows, :]
        return remote(source, cell.at[pl.ds(source_of(d) * own, own), z],
                      in_send.at[z, d - 1], in_recv.at[z, d - 1], comp=peer(d))

    def out_copy(z, d):
        to = peer(d)
        return remote(second.at[pl.ds(to * own, own), z], out.at[:, z, my_rows, :],
                      out_send.at[z, d - 1], out_recv.at[z, d - 1], comp=to)

    def out_arrival(z, d):
        rows_from = pl.ds(pl.multiple_of(source_of(d) * rows, rows), rows)
        return remote(second.at[pl.ds(me * own, own), z], out.at[:, z, rows_from, :],
                      out_send.at[z, d - 1], out_recv.at[z, d - 1], comp=peer(d))

    barrier = pltpu.get_barrier_semaphore()
    for d in range(1, n):
        pl.semaphore_signal(barrier, inc=1, device_id={"comp": peer(d)}, device_id_type=MESH)

    @pl.when(has_left)
    def _():
        pl.semaphore_signal(barrier, inc=1, device_id={"space": side - 1}, device_id_type=MESH)

    @pl.when(has_right)
    def _():
        pl.semaphore_signal(barrier, inc=1, device_id={"space": side + 1}, device_id_type=MESH)

    for copy in smalls:
        copy.start()

    @pl.loop(0, layers)
    def _(z):
        load(z).start()

    pl.semaphore_wait(barrier, n - 1 + has_left.astype(jnp.int32) + has_right.astype(jnp.int32))

    @pl.when(has_right)
    def _():
        for copy in rim_copies():
            copy.start()

        @pl.loop(0, layers)
        def _(z):
            y1_copy(z, 0).start()

    @pl.when(has_left)
    def _():
        @pl.loop(0, layers)
        def _(z):
            y1_copy(z, 1).start()

    @pl.when(jnp.logical_not(has_left))
    def _():
        yone[0] = jnp.zeros_like(yone[0])
        ytwo[0] = jnp.zeros_like(ytwo[0])
        rim_rate[...] = jnp.zeros_like(rim_rate)
        rim_flag[...] = jnp.zeros_like(rim_flag)

    @pl.when(jnp.logical_not(has_right))
    def _():
        yone[1] = jnp.zeros_like(yone[1])
        ytwo[1] = jnp.zeros_like(ytwo[1])

    @pl.when(jnp.logical_not(has_low))
    def _():
        xrecv[0] = jnp.zeros_like(xrecv[0])

    @pl.when(jnp.logical_not(has_up))
    def _():
        xrecv[1] = jnp.zeros_like(xrecv[1])

    @pl.when(has_left)
    def _():
        for copy in rim_copies():
            copy.wait_recv()

    for copy in smalls:
        copy.wait()
    flags = flag[...].astype(jnp.float32)
    plus = rate[...] * flags
    minus = rate[...] * (1.0 - flags)
    rim = rim_flag[...].astype(jnp.float32)
    rim_plus = rim_rate[...] * rim
    rim_minus = rim_rate[...] * (1.0 - rim)
    row_index = lax.broadcasted_iota(jnp.int32, (nx, ny), 0)
    down_plus = jnp.where(row_index == 0, 0.0, pltpu.roll(plus[0], 1, 0))
    down_minus = jnp.where(row_index == 0, 0.0, pltpu.roll(minus[0], 1, 0))
    side_plus = pltpu.roll(jnp.concatenate([rim_plus, plus[1]], axis=1), 1, 1)[:, LANES:]
    side_minus = pltpu.roll(jnp.concatenate([rim_minus, minus[1]], axis=1), 1, 1)[:, LANES:]
    coefs[0] = down_plus
    coefs[1] = minus[0]
    coefs[2] = side_plus
    coefs[3] = minus[1]
    coefs[4] = down_minus + plus[0] + side_minus + plus[1]

    def build_weights():
        matrix = inverse[...]
        eye = (
            lax.broadcasted_iota(jnp.int32, matrix.shape, 0)
            == lax.broadcasted_iota(jnp.int32, matrix.shape, 1)
        ).astype(jnp.float32)
        carry = eye - jnp.dot(
            matrix, mixing[...], precision=highest, preferred_element_type=jnp.float32
        )
        parts = [carry, -matrix * affinity[...], -matrix * mineral[...], matrix]
        parts = [split(expand(part, rows)) for part in parts]
        for ref, chosen in (
            (weights_one, parts[:2]),
            (weights_two, parts[:3]),
            (weights_in, parts[3:]),
        ):
            high = [part[0] for part in chosen]
            low = [part[1] for part in chosen]
            ref[...] = jnp.concatenate(high + high + low, axis=1)

    def product(ref, values):
        pairs = [split(value) for value in values]
        high = [pair[0] for pair in pairs]
        low = [pair[1] for pair in pairs]
        data = jnp.concatenate(high + low + high, axis=0)
        return jnp.dot(ref[...], data, preferred_element_type=jnp.float32)

    width = min(256, ny)
    pieces = [pl.ds(start, width) for start in range(0, ny, width)]

    def speciate(z):
        for piece in pieces:
            begun = product(weights_in, [target[:, piece]])
            base[:, piece] = begun
            state[:, piece] = begun

        @pl.loop(0, NEWT - 1)
        def _(_step):
            for piece in pieces:
                s = state[:, piece]
                state[:, piece] = base[:, piece] + product(weights_one, [s, jnp.tanh(s)])

        kept[...] = state[...]

        @pl.loop(0, STIFF)
        def _(_step):
            for piece in pieces:
                s = state[:, piece]
                state[:, piece] = base[:, piece] + product(
                    weights_two, [s, jnp.tanh(s), jnp.tanh(2.0 * s)]
                )

        stiff = mask[z] > 0
        return [
            jnp.where(stiff, state[pl.ds(c * rows, rows), :], kept[pl.ds(c * rows, rows), :])
            for c in range(NC)
        ]

    def stage_a(z):
        @pl.when(has_left)
        def _():
            y1_copy(z, 0).wait_recv()

        @pl.when(has_right)
        def _():
            y1_copy(z, 1).wait_recv()

        load(z).wait()
        for c in range(own):
            u = conc[c, z]
            lower_row = jnp.where(row_index == 0, 0.0, pltpu.roll(u, 1, 0))
            upper_row = jnp.where(row_index == nx - 1, 0.0, pltpu.roll(u, nx - 1, 0))
            lower_col, upper_col = shift_cols(u, yone[0, c, z], yone[1, c, z])
            component = me * own + c
            moved[c, z] = stencil(
                u, lower_row, upper_row, lower_col, upper_col,
                [coefs[k] for k in range(5)], spread[component], retard[component],
            )
        for d in range(1, n):
            in_copy(z, d).start()

    def stage_b(z):
        for d in range(1, n):
            in_arrival(z, d).wait_recv()
        for c in range(NC):
            target[pl.ds(c * rows, rows), :] = cell[c, z]
        for c in range(own):
            spot = pl.multiple_of((me * own + c) * rows, rows)
            target[pl.ds(spot, rows), :] = moved[c, z, my_rows, :]
        done = speciate(z)
        for c in range(NC):
            first[c, z] = done[c]
            xsend[0, z, pl.ds(c, 1), :] = done[c][rows - 1 : rows]
            xsend[1, z, pl.ds(c, 1), :] = done[c][:1]

        @pl.when(has_up)
        def _():
            x_copy(z, 0).start()

        @pl.when(has_low)
        def _():
            x_copy(z, 1).start()

        @pl.when(has_right)
        def _():
            y2_copy(z, 0).start()

        @pl.when(has_left)
        def _():
            y2_copy(z, 1).start()

    def stage_c(z):
        @pl.when(has_low)
        def _():
            x_copy(z, 0).wait_recv()

        @pl.when(has_up)
        def _():
            x_copy(z, 1).wait_recv()

        @pl.when(has_left)
        def _():
            y2_copy(z, 0).wait_recv()

        @pl.when(has_right)
        def _():
            y2_copy(z, 1).wait_recv()

        local = lax.broadcasted_iota(jnp.int32, (rows, ny), 0)
        for c in range(NC):
            u = first[c, z]
            below = jnp.broadcast_to(xrecv[0, z, pl.ds(c, 1), :], u.shape)
            above = jnp.broadcast_to(xrecv[1, z, pl.ds(c, 1), :], u.shape)
            lower_row = jnp.where(local == 0, below, pltpu.roll(u, 1, 0))
            upper_row = jnp.where(local == rows - 1, above, pltpu.roll(u, rows - 1, 0))
            lower_col, upper_col = shift_cols(u, ytwo[0, c, z], ytwo[1, c, z])
            target[pl.ds(c * rows, rows), :] = stencil(
                u, lower_row, upper_row, lower_col, upper_col,
                [coefs[k, my_rows, :] for k in range(5)], spread[c], retard[c],
            )
        done = speciate(z)
        for c in range(NC):
            second[c, z] = done[c]
        for d in range(1, n):
            out_copy(z, d).start()
        for c in range(own):
            out[c, z, my_rows, :] = second[me * own + c, z]

    @pl.loop(0, layers + AHEAD + BEHIND)
    def _(i):
        @pl.when(i < layers)
        def _():
            stage_a(i)

        @pl.when(i == AHEAD - 1)
        def _():
            build_weights()

        @pl.when((i >= AHEAD) & (i < layers + AHEAD))
        def _():
            stage_b(i - AHEAD)

        @pl.when(i >= AHEAD + BEHIND)
        def _():
            stage_c(i - AHEAD - BEHIND)

    @pl.loop(0, layers)
    def _(z):
        for d in range(1, n):
            out_arrival(z, d).wait_recv()
            in_copy(z, d).wait_send()
            out_copy(z, d).wait_send()

    @pl.when(has_right)
    def _():
        for copy in rim_copies():
            copy.wait_send()

        @pl.loop(0, layers)
        def _(z):
            y1_copy(z, 0).wait_send()
            y2_copy(z, 0).wait_send()

    @pl.when(has_left)
    def _():
        @pl.loop(0, layers)
        def _(z):
            y1_copy(z, 1).wait_send()
            y2_copy(z, 1).wait_send()

    @pl.when(has_up)
    def _():
        @pl.loop(0, layers)
        def _(z):
            x_copy(z, 0).wait_send()

    @pl.when(has_low)
    def _():
        @pl.loop(0, layers)
        def _(z):
            x_copy(z, 1).wait_send()


def fused_shards(
    n, wide, concentration, face_rate, face_flag, retardation, dispersion,
    mixing, mixing_inverse, affinity, mineral, stiff_mask,
):
    planes, nx, ny = concentration.shape
    own = planes // NZ
    rows = stiff_mask.shape[1]
    size = NC * rows
    f32, bf16 = jnp.float32, jnp.bfloat16
    vmem = pl.BlockSpec(memory_space=pltpu.VMEM)
    smem = pl.BlockSpec(memory_space=pltpu.SMEM)
    hbm = pl.BlockSpec(memory_space=pl.ANY)
    dma = pltpu.SemaphoreType.DMA
    result = pl.pallas_call(
        functools.partial(fused_kernel, n, wide),
        out_shape=pltpu.VMEM((own, NZ, nx, ny), f32),
        in_specs=[hbm, hbm, hbm, smem, smem, vmem, vmem, vmem, vmem, hbm],
        out_specs=vmem,
        scratch_shapes=[
            pltpu.VMEM((own, NZ, nx, ny), f32),
            pltpu.VMEM(face_rate.shape, f32),
            pltpu.VMEM(face_flag.shape, jnp.int32),
            pltpu.VMEM(stiff_mask.shape, jnp.int32),
            pltpu.VMEM((own, NZ, nx, ny), f32),
            pltpu.VMEM((NC, NZ, rows, ny), f32),
            pltpu.VMEM((NC, NZ, rows, ny), f32),
            pltpu.VMEM((NC, NZ, rows, ny), f32),
            pltpu.VMEM((2, NZ, NC, ny), f32),
            pltpu.VMEM((2, NZ, NC, ny), f32),
            pltpu.VMEM((2, own, NZ, nx, LANES), f32),
            pltpu.VMEM((2, NC, NZ, rows, LANES), f32),
            pltpu.VMEM((nx, LANES), f32),
            pltpu.VMEM((nx, LANES), jnp.int32),
            pltpu.VMEM((5, nx, ny), f32),
            pltpu.VMEM((size, 3 * size), bf16),
            pltpu.VMEM((size, 6 * size), bf16),
            pltpu.VMEM((size, 9 * size), bf16),
            pltpu.VMEM((size, ny), f32),
            pltpu.VMEM((size, ny), f32),
            pltpu.VMEM((size, ny), f32),
            pltpu.VMEM((size, ny), f32),
            dma((NZ, n - 1)), dma((NZ, n - 1)),
            dma((NZ, n - 1)), dma((NZ, n - 1)),
            dma((2, NZ)), dma((2, NZ)),
            dma((2, NZ)), dma((2, NZ)),
            dma((2, NZ)), dma((2, NZ)),
            dma((2,)), dma((2,)),
            dma((NZ,)), dma((3,)),
        ],
        compiler_params=pltpu.CompilerParams(collective_id=0, has_side_effects=True),
    )(
        concentration.reshape(own, NZ, nx, ny), face_rate, face_flag, retardation, dispersion,
        mixing, mixing_inverse, affinity.reshape(1, NC), mineral.reshape(1, NC), stiff_mask,
    )
    return result.reshape(planes, nx, ny)


def shifted(shard, axis, by):
    devices = lax.axis_size(axis)
    pairs = [(i, i + by) for i in range(devices) if 0 <= i + by < devices]
    return lax.ppermute(shard, axis, pairs)


def extended(block, sides, width):
    for axis, dim in sides:
        count = lax.axis_size(axis)
        forward = [(i, i + 1) for i in range(count - 1)]
        backward = [(target, source) for source, target in forward]
        low = lax.ppermute(
            lax.slice_in_dim(block, block.shape[dim] - width, None, axis=dim), axis, forward
        )
        high = lax.ppermute(lax.slice_in_dim(block, 0, width, axis=dim), axis, backward)
        block = jnp.concatenate([low, block, high], axis=dim)
    return block


def shift_down(values, axis_index):
    size_along = values.shape[axis_index]
    zero_row = jnp.zeros_like(lax.slice_in_dim(values, 0, 1, axis=axis_index))
    kept = lax.slice_in_dim(values, 0, size_along - 1, axis=axis_index)
    return jnp.concatenate([zero_row, kept], axis=axis_index)


def face_weights(face_rate, face_flag):
    flag_values = face_flag.astype(jnp.float32)
    weight_plus = face_rate * flag_values
    weight_minus = face_rate * (1.0 - flag_values)
    return (weight_plus, weight_minus)


def advance(
    values, lower_row, upper_row, lower_col, upper_col, coefficients, retard_planes, spread_planes
):
    divergence = (
        coefficients[0] * lower_row
        + coefficients[1] * upper_row
        + coefficients[2] * lower_col
        + coefficients[3] * upper_col
        - coefficients[4] * values
    )
    laplace = lower_row + upper_row + lower_col + upper_col - 4.0 * values
    return values + (divergence + spread_planes * laplace) / retard_planes


def residual_of(species, target, mixing, affinity, mineral, stiff):
    total = jnp.dot(
        mixing, species, precision=highest, preferred_element_type=jnp.float32
    ) + affinity[:, None] * jnp.tanh(species)
    if stiff:
        total = total + mineral[:, None] * jnp.tanh(2.0 * species)
    return total - target


def newton_steps(species, target, repeats, stiff, mixing, mixing_inverse, affinity, mineral):
    for iteration in range(repeats):
        update = residual_of(species, target, mixing, affinity, mineral, stiff)
        species = species - jnp.dot(
            mixing_inverse, update, precision=highest, preferred_element_type=jnp.float32
        )
    return species


def speciate(cell_block, stiff_mask, mixing, mixing_inverse, affinity, mineral):
    target = cell_block.reshape(NC, -1)
    flat_mask = stiff_mask.reshape(-1) > 0
    species = jnp.zeros_like(target)
    species = newton_steps(species, target, NEWT, False, mixing, mixing_inverse, affinity, mineral)
    stiffer = newton_steps(species, target, STIFF, True, mixing, mixing_inverse, affinity, mineral)
    species = jnp.where(flat_mask[None, :], stiffer, species)
    return species.reshape(cell_block.shape)


def shards(
    concentration,
    face_rate,
    face_flag,
    retardation,
    dispersion,
    mixing,
    mixing_inverse,
    affinity,
    mineral,
    stiff_mask,
):
    weight_plus, weight_minus = face_weights(face_rate, face_flag)
    rim_weights = jnp.stack([weight_plus[1, :, -1], weight_minus[1, :, -1]])
    left_rims = shifted(rim_weights, "space", 1)
    side_plus = jnp.concatenate([left_rims[0][:, None], weight_plus[1, :, :-1]], axis=1)
    side_minus = jnp.concatenate([left_rims[1][:, None], weight_minus[1, :, :-1]], axis=1)
    down_plus = shift_down(weight_plus[0], 0)
    down_minus = shift_down(weight_minus[0], 0)
    centre = down_minus + weight_plus[0] + side_minus + weight_plus[1]
    coefficients = jnp.stack([down_plus, weight_minus[0], side_plus, weight_minus[1], centre])
    retard_all = jnp.repeat(retardation, NZ)
    spread_all = jnp.repeat(dispersion, NZ)
    rows_held = stiff_mask.shape[1]
    row_start = lax.axis_index("comp") * rows_held
    cell_coefficients = lax.dynamic_slice_in_dim(coefficients, row_start, rows_held, 1)
    retard_planes = retard_all[:, None, None]
    spread_planes = spread_all[:, None, None]
    cell_block = lax.all_to_all(concentration, "comp", split_axis=1, concat_axis=0, tiled=True)
    for step_index in range(STEPS):
        padded = extended(cell_block, (("comp", 1), ("space", 2)), 1)
        cell_block = advance(
            cell_block,
            padded[:, :-2, 1:-1],
            padded[:, 2:, 1:-1],
            padded[:, 1:-1, :-2],
            padded[:, 1:-1, 2:],
            cell_coefficients,
            retard_planes,
            spread_planes,
        )
        cell_block = speciate(cell_block, stiff_mask, mixing, mixing_inverse, affinity, mineral)
    return lax.all_to_all(cell_block, "comp", split_axis=0, concat_axis=1, tiled=True)


def solution(mesh):
    in_specs = (
        P(("real", "comp"), None, "space"),
        P(None, "real", "space"),
        P(None, "real", "space"),
        P(),
        P(),
        P(),
        P(),
        P(),
        P(),
        P(None, ("real", "comp"), "space"),
    )
    out_specs = P(("real", "comp"), None, "space")
    n, wide = mesh.shape["comp"], mesh.shape["space"]
    body = functools.partial(fused_shards, n, wide) if NC % n == 0 else shards
    return jax.shard_map(body, mesh=mesh, in_specs=in_specs, out_specs=out_specs, check_vma=False)
```

```python
import functools

import jax
import jax.numpy as jnp
from jax import lax
from jax.experimental import pallas as pl
from jax.experimental.pallas import tpu as pltpu
from jax.sharding import PartitionSpec as P

NC = 16
NZ = 8
STEPS = 2
NEWT = 4
STIFF = 4
LANES = 128
AHEAD = 3
BEHIND = 2
MESH = pl.DeviceIdType.MESH

highest = lax.Precision.HIGHEST


def split(value):
    high = value.astype(jnp.bfloat16)
    low = (value - high.astype(jnp.float32)).astype(jnp.bfloat16)
    return high, low


def expand(small, rows):
    count = small.shape[0]
    size = count * rows
    tall = (
        lax.broadcasted_iota(jnp.int32, (size, count), 0) // rows
        == lax.broadcasted_iota(jnp.int32, (size, count), 1)
    ).astype(jnp.float32)
    wide = (
        lax.broadcasted_iota(jnp.int32, (count, size), 1) // rows
        == lax.broadcasted_iota(jnp.int32, (count, size), 0)
    ).astype(jnp.float32)
    dot = functools.partial(jnp.dot, precision=highest, preferred_element_type=jnp.float32)
    full = dot(dot(tall, small), wide)
    same = (
        lax.broadcasted_iota(jnp.int32, (size, size), 0) % rows
        == lax.broadcasted_iota(jnp.int32, (size, size), 1) % rows
    )
    return jnp.where(same, full, 0.0)


def shift_cols(values, left, right):
    columns = values.shape[1]
    lower = pltpu.roll(jnp.concatenate([left, values], axis=1), 1, 1)[:, LANES:]
    upper = pltpu.roll(
        jnp.concatenate([values, right], axis=1), columns + LANES - 1, 1
    )[:, :columns]
    return lower, upper


def stencil(values, lower_row, upper_row, lower_col, upper_col, coefs, spread, retard):
    inverse = 1.0 / jnp.full((1, values.shape[1]), retard, jnp.float32)
    moved = (
        (coefs[0] + spread) * lower_row
        + (coefs[1] + spread) * upper_row
        + (coefs[2] + spread) * lower_col
        + (coefs[3] + spread) * upper_col
        - (coefs[4] + 4.0 * spread) * values
    )
    return values + moved * inverse


def fused_kernel(
    n,
    wide,
    conc_hbm,
    rate_hbm,
    flag_hbm,
    retard,
    spread,
    mixing,
    inverse,
    affinity,
    mineral,
    mask_hbm,
    out,
    conc,
    rate,
    flag,
    mask,
    moved,
    cell,
    first,
    second,
    xsend,
    xrecv,
    yone,
    ytwo,
    rim_rate,
    rim_flag,
    coefs,
    weights_in,
    weights_one,
    weights_two,
    target,
    state,
    base,
    kept,
    in_send,
    in_recv,
    out_send,
    out_recv,
    x_send,
    x_recv,
    y1_send,
    y1_recv,
    y2_send,
    y2_recv,
    r_send,
    r_recv,
    load_sem,
    small_sem,
    edge_send,
    edge_recv,
):
    own, layers, nx, ny = conc.shape
    rows = mask.shape[1]
    me = lax.axis_index("comp")
    side = lax.axis_index("space")
    has_left, has_right = side > 0, side < wide - 1
    has_low, has_up = me > 0, me < n - 1
    my_rows = pl.ds(pl.multiple_of(me * rows, rows), rows)

    def peer(d):
        if n == 4:
            return (lax.rem(me + 2, 4), 3 - me, me + 1 - 2 * lax.rem(me, 2))[d - 1]
        return lax.rem(me + d, n)

    def source_of(d):
        return peer(d) if n == 4 else lax.rem(me + n - d, n)

    def load(z):
        return pltpu.make_async_copy(conc_hbm.at[:, z], conc.at[:, z], load_sem.at[z])

    smalls = [
        pltpu.make_async_copy(rate_hbm, rate, small_sem.at[0]),
        pltpu.make_async_copy(flag_hbm, flag, small_sem.at[1]),
        pltpu.make_async_copy(mask_hbm, mask, small_sem.at[2]),
    ]

    def remote(src, dst, send, recv, **where):
        return pltpu.make_async_remote_copy(
            src_ref=src, dst_ref=dst, send_sem=send, recv_sem=recv,
            device_id=where, device_id_type=MESH,
        )

    def y1_copy(z, way):
        source = conc_hbm.at[:, z, :, pl.ds(ny - LANES if way == 0 else 0, LANES)]
        return remote(source, yone.at[way, :, z], y1_send.at[way, z], y1_recv.at[way, z],
                      space=side + (1 if way == 0 else -1))

    def y2_copy(z, way):
        source = first.at[:, z, :, pl.ds(ny - LANES if way == 0 else 0, LANES)]
        return remote(source, ytwo.at[way, :, z], y2_send.at[way, z], y2_recv.at[way, z],
                      space=side + (1 if way == 0 else -1))

    def x_copy(z, way):
        return remote(xsend.at[way, z], xrecv.at[way, z], x_send.at[way, z], x_recv.at[way, z],
                      comp=me + (1 if way == 0 else -1))

    def rim_copies():
        last = pl.ds(ny - LANES, LANES)
        return (
            remote(rate_hbm.at[1, :, last], rim_rate, r_send.at[0], r_recv.at[0], space=side + 1),
            remote(flag_hbm.at[1, :, last], rim_flag, r_send.at[1], r_recv.at[1], space=side + 1),
        )

    whole = pl.ds(0, ny)
    inner = pl.ds(LANES, ny - 2 * LANES)
    edges = (pl.ds(0, LANES), pl.ds(ny - LANES, LANES))

    def in_copy(z, d, columns, sems):
        to = peer(d)
        source = moved.at[:, z, pl.ds(pl.multiple_of(to * rows, rows), rows), columns]
        return remote(source, cell.at[pl.ds(me * own, own), z, :, columns], *sems, comp=to)

    def in_arrival(z, d, columns, sems):
        source = moved.at[:, z, my_rows, columns]
        return remote(source, cell.at[pl.ds(source_of(d) * own, own), z, :, columns],
                      *sems, comp=peer(d))

    def in_sems(z, d):
        return in_send.at[z, d - 1], in_recv.at[z, d - 1]

    def edge_sems(k, d):
        return edge_send.at[k, d - 1], edge_recv.at[k, d - 1]

    def out_copy(z, d):
        to = peer(d)
        return remote(second.at[pl.ds(to * own, own), z], out.at[:, z, my_rows, :],
                      out_send.at[z, d - 1], out_recv.at[z, d - 1], comp=to)

    def out_arrival(z, d):
        rows_from = pl.ds(pl.multiple_of(source_of(d) * rows, rows), rows)
        return remote(second.at[pl.ds(me * own, own), z], out.at[:, z, rows_from, :],
                      out_send.at[z, d - 1], out_recv.at[z, d - 1], comp=peer(d))

    barrier = pltpu.get_barrier_semaphore()
    for d in range(1, n):
        pl.semaphore_signal(barrier, inc=1, device_id={"comp": peer(d)}, device_id_type=MESH)

    @pl.when(has_left)
    def _():
        pl.semaphore_signal(barrier, inc=1, device_id={"space": side - 1}, device_id_type=MESH)

    @pl.when(has_right)
    def _():
        pl.semaphore_signal(barrier, inc=1, device_id={"space": side + 1}, device_id_type=MESH)

    for copy in smalls:
        copy.start()

    @pl.loop(0, layers)
    def _(z):
        load(z).start()

    @pl.when(jnp.logical_not(has_left))
    def _():
        yone[0] = jnp.zeros_like(yone[0])
        ytwo[0] = jnp.zeros_like(ytwo[0])
        rim_rate[...] = jnp.zeros_like(rim_rate)
        rim_flag[...] = jnp.zeros_like(rim_flag)

    @pl.when(jnp.logical_not(has_right))
    def _():
        yone[1] = jnp.zeros_like(yone[1])
        ytwo[1] = jnp.zeros_like(ytwo[1])

    @pl.when(jnp.logical_not(has_low))
    def _():
        xrecv[0] = jnp.zeros_like(xrecv[0])

    @pl.when(jnp.logical_not(has_up))
    def _():
        xrecv[1] = jnp.zeros_like(xrecv[1])

    for copy in smalls:
        copy.wait()
    flags = flag[...].astype(jnp.float32)
    plus = rate[...] * flags
    minus = rate[...] * (1.0 - flags)
    row_index = lax.broadcasted_iota(jnp.int32, (nx, ny), 0)
    column_index = lax.broadcasted_iota(jnp.int32, (nx, ny), 1)
    down_plus = jnp.where(row_index == 0, 0.0, pltpu.roll(plus[0], 1, 0))
    down_minus = jnp.where(row_index == 0, 0.0, pltpu.roll(minus[0], 1, 0))
    side_plus = jnp.where(column_index == 0, 0.0, pltpu.roll(plus[1], 1, 1))
    side_minus = jnp.where(column_index == 0, 0.0, pltpu.roll(minus[1], 1, 1))
    coefs[0] = down_plus
    coefs[1] = minus[0]
    coefs[2] = side_plus
    coefs[3] = minus[1]
    coefs[4] = down_minus + plus[0] + side_minus + plus[1]

    def carry_planes(z, columns, left_of, right_of):
        count = columns.size
        index = lax.broadcasted_iota(jnp.int32, (nx, count), 0)
        for c in range(own):
            u = conc[c, z, :, columns]
            lower_row = jnp.where(index == 0, 0.0, pltpu.roll(u, 1, 0))
            upper_row = jnp.where(index == nx - 1, 0.0, pltpu.roll(u, nx - 1, 0))
            lower_col, upper_col = shift_cols(u, left_of(c), right_of(c))
            component = me * own + c
            moved[c, z, :, columns] = stencil(
                u, lower_row, upper_row, lower_col, upper_col,
                [coefs[k, :, columns] for k in range(5)], spread[component], retard[component],
            )

    def carry_inner(z):
        carry_planes(
            z, inner,
            lambda c: conc[c, z, :, pl.ds(0, LANES)],
            lambda c: conc[c, z, :, pl.ds(ny - LANES, LANES)],
        )

    def carry_edges(z):
        carry_planes(
            z, edges[0],
            lambda c: yone[0, c, z],
            lambda c: conc[c, z, :, pl.ds(LANES, LANES)],
        )
        carry_planes(
            z, edges[1],
            lambda c: conc[c, z, :, pl.ds(ny - 2 * LANES, LANES)],
            lambda c: yone[1, c, z],
        )

    load(0).wait()
    carry_inner(0)

    pl.semaphore_wait(barrier, n - 1 + has_left.astype(jnp.int32) + has_right.astype(jnp.int32))

    @pl.when(has_right)
    def _():
        for copy in rim_copies():
            copy.start()

        @pl.loop(0, layers)
        def _(z):
            y1_copy(z, 0).start()

    @pl.when(has_left)
    def _():
        @pl.loop(0, layers)
        def _(z):
            y1_copy(z, 1).start()

    for d in range(1, n):
        in_copy(0, d, inner, in_sems(0, d)).start()

    @pl.when(has_left)
    def _():
        for copy in rim_copies():
            copy.wait_recv()

    rim = rim_flag[...].astype(jnp.float32)
    at_rim = lax.broadcasted_iota(jnp.int32, (nx, LANES), 1) == 0
    rim_plus = pltpu.roll(rim_rate[...] * rim, 1, 1)
    rim_minus = pltpu.roll(rim_rate[...] * (1.0 - rim), 1, 1)
    coefs[2, :, edges[0]] = coefs[2, :, edges[0]] + jnp.where(at_rim, rim_plus, 0.0)
    coefs[4, :, edges[0]] = coefs[4, :, edges[0]] + jnp.where(at_rim, rim_minus, 0.0)

    def build_weights():
        matrix = inverse[...]
        eye = (
            lax.broadcasted_iota(jnp.int32, matrix.shape, 0)
            == lax.broadcasted_iota(jnp.int32, matrix.shape, 1)
        ).astype(jnp.float32)
        carry = eye - jnp.dot(
            matrix, mixing[...], precision=highest, preferred_element_type=jnp.float32
        )
        parts = [carry, -matrix * affinity[...], -matrix * mineral[...], matrix]
        parts = [split(expand(part, rows)) for part in parts]
        for ref, chosen in (
            (weights_one, parts[:2]),
            (weights_two, parts[:3]),
            (weights_in, parts[3:]),
        ):
            high = [part[0] for part in chosen]
            low = [part[1] for part in chosen]
            ref[...] = jnp.concatenate(high + high + low, axis=1)

    def product(ref, values):
        pairs = [split(value) for value in values]
        high = [pair[0] for pair in pairs]
        low = [pair[1] for pair in pairs]
        data = jnp.concatenate(high + low + high, axis=0)
        return jnp.dot(ref[...], data, preferred_element_type=jnp.float32)

    width = min(256, ny)
    pieces = [pl.ds(start, width) for start in range(0, ny, width)]

    def speciate(z):
        for piece in pieces:
            begun = product(weights_in, [target[:, piece]])
            base[:, piece] = begun
            state[:, piece] = begun

        @pl.loop(0, NEWT - 1)
        def _(_step):
            for piece in pieces:
                s = state[:, piece]
                state[:, piece] = base[:, piece] + product(weights_one, [s, jnp.tanh(s)])

        kept[...] = state[...]

        @pl.loop(0, STIFF)
        def _(_step):
            for piece in pieces:
                s = state[:, piece]
                state[:, piece] = base[:, piece] + product(
                    weights_two, [s, jnp.tanh(s), jnp.tanh(2.0 * s)]
                )

        stiff = mask[z] > 0
        return [
            jnp.where(stiff, state[pl.ds(c * rows, rows), :], kept[pl.ds(c * rows, rows), :])
            for c in range(NC)
        ]

    def wait_slabs(z):
        @pl.when(has_left)
        def _():
            y1_copy(z, 0).wait_recv()

        @pl.when(has_right)
        def _():
            y1_copy(z, 1).wait_recv()

    def stage_a_first():
        wait_slabs(0)
        carry_edges(0)
        for d in range(1, n):
            for k in range(2):
                in_copy(0, d, edges[k], edge_sems(k, d)).start()

    def stage_a(z):
        load(z).wait()
        carry_inner(z)
        wait_slabs(z)
        carry_edges(z)
        for d in range(1, n):
            in_copy(z, d, whole, in_sems(z, d)).start()

    def stage_b(z):
        @pl.when(z == 0)
        def _():
            for d in range(1, n):
                in_arrival(0, d, inner, in_sems(0, d)).wait_recv()
                for k in range(2):
                    in_arrival(0, d, edges[k], edge_sems(k, d)).wait_recv()

        @pl.when(z > 0)
        def _():
            for d in range(1, n):
                in_arrival(z, d, whole, in_sems(z, d)).wait_recv()

        for c in range(NC):
            target[pl.ds(c * rows, rows), :] = cell[c, z]
        for c in range(own):
            spot = pl.multiple_of((me * own + c) * rows, rows)
            target[pl.ds(spot, rows), :] = moved[c, z, my_rows, :]
        done = speciate(z)
        for c in range(NC):
            first[c, z] = done[c]
            xsend[0, z, pl.ds(c, 1), :] = done[c][rows - 1 : rows]
            xsend[1, z, pl.ds(c, 1), :] = done[c][:1]

        @pl.when(has_up)
        def _():
            x_copy(z, 0).start()

        @pl.when(has_low)
        def _():
            x_copy(z, 1).start()

        @pl.when(has_right)
        def _():
            y2_copy(z, 0).start()

        @pl.when(has_left)
        def _():
            y2_copy(z, 1).start()

    def stage_c(z):
        @pl.when(has_low)
        def _():
            x_copy(z, 0).wait_recv()

        @pl.when(has_up)
        def _():
            x_copy(z, 1).wait_recv()

        @pl.when(has_left)
        def _():
            y2_copy(z, 0).wait_recv()

        @pl.when(has_right)
        def _():
            y2_copy(z, 1).wait_recv()

        local = lax.broadcasted_iota(jnp.int32, (rows, ny), 0)
        for c in range(NC):
            u = first[c, z]
            below = jnp.broadcast_to(xrecv[0, z, pl.ds(c, 1), :], u.shape)
            above = jnp.broadcast_to(xrecv[1, z, pl.ds(c, 1), :], u.shape)
            lower_row = jnp.where(local == 0, below, pltpu.roll(u, 1, 0))
            upper_row = jnp.where(local == rows - 1, above, pltpu.roll(u, rows - 1, 0))
            lower_col, upper_col = shift_cols(u, ytwo[0, c, z], ytwo[1, c, z])
            target[pl.ds(c * rows, rows), :] = stencil(
                u, lower_row, upper_row, lower_col, upper_col,
                [coefs[k, my_rows, :] for k in range(5)], spread[c], retard[c],
            )
        done = speciate(z)
        for c in range(NC):
            second[c, z] = done[c]
        for d in range(1, n):
            out_copy(z, d).start()
        for c in range(own):
            out[c, z, my_rows, :] = second[me * own + c, z]

    @pl.loop(0, layers + AHEAD + BEHIND)
    def _(i):
        @pl.when(i == 0)
        def _():
            stage_a_first()

        @pl.when((i > 0) & (i < layers))
        def _():
            stage_a(i)

        @pl.when(i == AHEAD - 1)
        def _():
            build_weights()

        @pl.when((i >= AHEAD) & (i < layers + AHEAD))
        def _():
            stage_b(i - AHEAD)

        @pl.when(i >= AHEAD + BEHIND)
        def _():
            stage_c(i - AHEAD - BEHIND)

    @pl.loop(0, layers)
    def _(z):
        for d in range(1, n):
            out_arrival(z, d).wait_recv()
            out_copy(z, d).wait_send()

    for d in range(1, n):
        in_copy(0, d, inner, in_sems(0, d)).wait_send()
        for k in range(2):
            in_copy(0, d, edges[k], edge_sems(k, d)).wait_send()

    @pl.loop(1, layers)
    def _(z):
        for d in range(1, n):
            in_copy(z, d, whole, in_sems(z, d)).wait_send()

    @pl.when(has_right)
    def _():
        for copy in rim_copies():
            copy.wait_send()

        @pl.loop(0, layers)
        def _(z):
            y1_copy(z, 0).wait_send()
            y2_copy(z, 0).wait_send()

    @pl.when(has_left)
    def _():
        @pl.loop(0, layers)
        def _(z):
            y1_copy(z, 1).wait_send()
            y2_copy(z, 1).wait_send()

    @pl.when(has_up)
    def _():
        @pl.loop(0, layers)
        def _(z):
            x_copy(z, 0).wait_send()

    @pl.when(has_low)
    def _():
        @pl.loop(0, layers)
        def _(z):
            x_copy(z, 1).wait_send()


def fused_shards(
    n, wide, concentration, face_rate, face_flag, retardation, dispersion,
    mixing, mixing_inverse, affinity, mineral, stiff_mask,
):
    planes, nx, ny = concentration.shape
    if NC % n or ny < 4 * LANES:
        return shards(
            concentration, face_rate, face_flag, retardation, dispersion,
            mixing, mixing_inverse, affinity, mineral, stiff_mask,
        )
    own = planes // NZ
    rows = stiff_mask.shape[1]
    size = NC * rows
    f32, bf16 = jnp.float32, jnp.bfloat16
    vmem = pl.BlockSpec(memory_space=pltpu.VMEM)
    smem = pl.BlockSpec(memory_space=pltpu.SMEM)
    hbm = pl.BlockSpec(memory_space=pl.ANY)
    dma = pltpu.SemaphoreType.DMA
    result = pl.pallas_call(
        functools.partial(fused_kernel, n, wide),
        out_shape=pltpu.VMEM((own, NZ, nx, ny), f32),
        in_specs=[hbm, hbm, hbm, smem, smem, vmem, vmem, vmem, vmem, hbm],
        out_specs=vmem,
        scratch_shapes=[
            pltpu.VMEM((own, NZ, nx, ny), f32),
            pltpu.VMEM(face_rate.shape, f32),
            pltpu.VMEM(face_flag.shape, jnp.int32),
            pltpu.VMEM(stiff_mask.shape, jnp.int32),
            pltpu.VMEM((own, NZ, nx, ny), f32),
            pltpu.VMEM((NC, NZ, rows, ny), f32),
            pltpu.VMEM((NC, NZ, rows, ny), f32),
            pltpu.VMEM((NC, NZ, rows, ny), f32),
            pltpu.VMEM((2, NZ, NC, ny), f32),
            pltpu.VMEM((2, NZ, NC, ny), f32),
            pltpu.VMEM((2, own, NZ, nx, LANES), f32),
            pltpu.VMEM((2, NC, NZ, rows, LANES), f32),
            pltpu.VMEM((nx, LANES), f32),
            pltpu.VMEM((nx, LANES), jnp.int32),
            pltpu.VMEM((5, nx, ny), f32),
            pltpu.VMEM((size, 3 * size), bf16),
            pltpu.VMEM((size, 6 * size), bf16),
            pltpu.VMEM((size, 9 * size), bf16),
            pltpu.VMEM((size, ny), f32),
            pltpu.VMEM((size, ny), f32),
            pltpu.VMEM((size, ny), f32),
            pltpu.VMEM((size, ny), f32),
            dma((NZ, n - 1)), dma((NZ, n - 1)),
            dma((NZ, n - 1)), dma((NZ, n - 1)),
            dma((2, NZ)), dma((2, NZ)),
            dma((2, NZ)), dma((2, NZ)),
            dma((2, NZ)), dma((2, NZ)),
            dma((2,)), dma((2,)),
            dma((NZ,)), dma((3,)),
            dma((2, n - 1)), dma((2, n - 1)),
        ],
        compiler_params=pltpu.CompilerParams(collective_id=0, has_side_effects=True),
    )(
        concentration.reshape(own, NZ, nx, ny), face_rate, face_flag, retardation, dispersion,
        mixing, mixing_inverse, affinity.reshape(1, NC), mineral.reshape(1, NC), stiff_mask,
    )
    return result.reshape(planes, nx, ny)


def shifted(shard, axis, by):
    devices = lax.axis_size(axis)
    pairs = [(i, i + by) for i in range(devices) if 0 <= i + by < devices]
    return lax.ppermute(shard, axis, pairs)


def extended(block, sides, width):
    for axis, dim in sides:
        count = lax.axis_size(axis)
        forward = [(i, i + 1) for i in range(count - 1)]
        backward = [(target, source) for source, target in forward]
        low = lax.ppermute(
            lax.slice_in_dim(block, block.shape[dim] - width, None, axis=dim), axis, forward
        )
        high = lax.ppermute(lax.slice_in_dim(block, 0, width, axis=dim), axis, backward)
        block = jnp.concatenate([low, block, high], axis=dim)
    return block


def shift_down(values, axis_index):
    size_along = values.shape[axis_index]
    zero_row = jnp.zeros_like(lax.slice_in_dim(values, 0, 1, axis=axis_index))
    kept = lax.slice_in_dim(values, 0, size_along - 1, axis=axis_index)
    return jnp.concatenate([zero_row, kept], axis=axis_index)


def face_weights(face_rate, face_flag):
    flag_values = face_flag.astype(jnp.float32)
    weight_plus = face_rate * flag_values
    weight_minus = face_rate * (1.0 - flag_values)
    return (weight_plus, weight_minus)


def advance(
    values, lower_row, upper_row, lower_col, upper_col, coefficients, retard_planes, spread_planes
):
    divergence = (
        coefficients[0] * lower_row
        + coefficients[1] * upper_row
        + coefficients[2] * lower_col
        + coefficients[3] * upper_col
        - coefficients[4] * values
    )
    laplace = lower_row + upper_row + lower_col + upper_col - 4.0 * values
    return values + (divergence + spread_planes * laplace) / retard_planes


def residual_of(species, target, mixing, affinity, mineral, stiff):
    total = jnp.dot(
        mixing, species, precision=highest, preferred_element_type=jnp.float32
    ) + affinity[:, None] * jnp.tanh(species)
    if stiff:
        total = total + mineral[:, None] * jnp.tanh(2.0 * species)
    return total - target


def newton_steps(species, target, repeats, stiff, mixing, mixing_inverse, affinity, mineral):
    for iteration in range(repeats):
        update = residual_of(species, target, mixing, affinity, mineral, stiff)
        species = species - jnp.dot(
            mixing_inverse, update, precision=highest, preferred_element_type=jnp.float32
        )
    return species


def speciate(cell_block, stiff_mask, mixing, mixing_inverse, affinity, mineral):
    target = cell_block.reshape(NC, -1)
    flat_mask = stiff_mask.reshape(-1) > 0
    species = jnp.zeros_like(target)
    species = newton_steps(species, target, NEWT, False, mixing, mixing_inverse, affinity, mineral)
    stiffer = newton_steps(species, target, STIFF, True, mixing, mixing_inverse, affinity, mineral)
    species = jnp.where(flat_mask[None, :], stiffer, species)
    return species.reshape(cell_block.shape)


def shards(
    concentration,
    face_rate,
    face_flag,
    retardation,
    dispersion,
    mixing,
    mixing_inverse,
    affinity,
    mineral,
    stiff_mask,
):
    weight_plus, weight_minus = face_weights(face_rate, face_flag)
    rim_weights = jnp.stack([weight_plus[1, :, -1], weight_minus[1, :, -1]])
    left_rims = shifted(rim_weights, "space", 1)
    side_plus = jnp.concatenate([left_rims[0][:, None], weight_plus[1, :, :-1]], axis=1)
    side_minus = jnp.concatenate([left_rims[1][:, None], weight_minus[1, :, :-1]], axis=1)
    down_plus = shift_down(weight_plus[0], 0)
    down_minus = shift_down(weight_minus[0], 0)
    centre = down_minus + weight_plus[0] + side_minus + weight_plus[1]
    coefficients = jnp.stack([down_plus, weight_minus[0], side_plus, weight_minus[1], centre])
    retard_all = jnp.repeat(retardation, NZ)
    spread_all = jnp.repeat(dispersion, NZ)
    rows_held = stiff_mask.shape[1]
    row_start = lax.axis_index("comp") * rows_held
    cell_coefficients = lax.dynamic_slice_in_dim(coefficients, row_start, rows_held, 1)
    retard_planes = retard_all[:, None, None]
    spread_planes = spread_all[:, None, None]
    cell_block = lax.all_to_all(concentration, "comp", split_axis=1, concat_axis=0, tiled=True)
    for step_index in range(STEPS):
        padded = extended(cell_block, (("comp", 1), ("space", 2)), 1)
        cell_block = advance(
            cell_block,
            padded[:, :-2, 1:-1],
            padded[:, 2:, 1:-1],
            padded[:, 1:-1, :-2],
            padded[:, 1:-1, 2:],
            cell_coefficients,
            retard_planes,
            spread_planes,
        )
        cell_block = speciate(cell_block, stiff_mask, mixing, mixing_inverse, affinity, mineral)
    return lax.all_to_all(cell_block, "comp", split_axis=0, concat_axis=1, tiled=True)


def solution(mesh):
    in_specs = (
        P(("real", "comp"), None, "space"),
        P(None, "real", "space"),
        P(None, "real", "space"),
        P(),
        P(),
        P(),
        P(),
        P(),
        P(),
        P(None, ("real", "comp"), "space"),
    )
    out_specs = P(("real", "comp"), None, "space")
    n, wide = mesh.shape["comp"], mesh.shape["space"]
    body = functools.partial(fused_shards, n, wide)
    return jax.shard_map(body, mesh=mesh, in_specs=in_specs, out_specs=out_specs, check_vma=False)
```
